512 devices in a mesh: dp: 32 (over z, y_lo, core), tensor: 16 (over y_hi, x).
Axes of the slice: x: 4, y: 8 (y_hi: 4, y_lo: 2; y = y_hi * 2 + y_lo), z: 8, core: 2. Of those that a mesh axis runs over, the one named last changes fastest.
Arguments:
- tokens: bfloat16 [8192, 4096], P(('dp', 'tensor')), may hold values from -6 to 6
- norm_gain: float32 [4096], replicated, may hold values from 0.1 to 1.9
- gate_tiles: bfloat16 [16, 32, 16, 4096], P('tensor', 'dp'), may hold values from -0.125 to 0.125
- up_tiles: bfloat16 [16, 32, 16, 4096], P('tensor', 'dp'), may hold values from -0.125 to 0.125
- down_tiles: bfloat16 [16, 32, 16, 4096], P('tensor', 'dp'), may hold values from -0.0625 to 0.0625
- tile_ids: int32 [16, 32, 3, 16], P('tensor', 'dp'), may hold values from 0 to 27, as said below
- tile_counts: int32 [16, 32, 3], P('tensor', 'dp'), may hold values from 8 to 16, as said below
Outputs:
- mixed: bfloat16 [8192, 4096], P(('dp', 'tensor'))
The draws below stay inside these ranges and needn't reach their ends.
Inputs may be any that keep to these rules, and one draw needn't show every extreme that they name: `tile_ids`: each device's slots of one matrix name distinct tiles of its shard; local tile l lies in tile row l // 14 and tile column l % 14 of the shard. `tile_counts`: only the first count slots of a matrix on a device hold kept tiles; for each matrix some device has all 16 slots kept.
All inputs are finite; a program needn't handle non-finite values.
Results may differ from the reference program's by a relative error of at most 0.014.
Values may be sent and summed in bfloat16 or wider, within the bound.
No kernel may reach another device: no remote copies, remote signals or barrier semaphores. Data moves between devices by JAX's collectives and lax.ppermute only.
A program may use at most 128 MiB of HBM per device.

```python
import jax
import jax.numpy as jnp
from jax import lax

D = 4096
FF = 14336
TILE = 64
TOKENS = 8192
ROW_TILES = 2
COL_TILES = 14
LOCAL = 28
KCAP = 16
N_DP = 32
N_TENSOR = 16


def draw_tile_ids(key, part):
    scores = jax.random.randint(key, (N_TENSOR, N_DP, 3, LOCAL), 0, 1 << 20) * LOCAL + jnp.arange(LOCAL)
    order = jnp.argsort(scores, axis=-1, stable=True)
    return order[..., :KCAP].astype(jnp.int32)


def draw_tile_counts(key, part):
    lowest = max(1, KCAP // 2)
    counts = jax.random.randint(key, (N_TENSOR * N_DP, 3), lowest, KCAP + 1)
    chosen = jax.random.randint(jax.random.fold_in(key, 7), (3,), 0, N_TENSOR * N_DP)
    hit = jnp.arange(N_TENSOR * N_DP)[:, None] == chosen[None, :]
    counts = jnp.where(hit, KCAP, counts)
    return counts.reshape(N_TENSOR, N_DP, 3).astype(jnp.int32)


def block_levels(stream_key, shape, split, least, high):
    def one(position, shards_of):
        draws = jax.random.uniform(jax.random.fold_in(jax.random.fold_in(stream_key, 6), position), (shards_of,), jnp.float32, least / len(split), high / len(split))
        return jnp.repeat(jnp.exp(draws), shape[position] // shards_of).reshape((-1,) + (1,) * (len(shape) - position - 1))

    level = one(*split[0])
    for cut in split[1:]:
        level = level * one(*cut)
    return level


def normal_values(key, dims, deviation, reach, shards=(), dtype=jnp.bfloat16):
    drawn = jax.random.normal(key, dims, jnp.float32) * deviation
    if len(shards) > 0:
        drawn = block_levels(key, dims, shards, -0.22, 0.18) * drawn
    return jnp.clip(drawn, min=-reach, max=reach).astype(dtype)


def setup_inputs(seed: int = 0) -> dict:
    keys = jax.random.split(jax.random.key(seed), 8)
    return {
        "tokens": normal_values(keys[0], (TOKENS, D), 1.0, 6.0, ((0, 512),)),
        "norm_gain": jnp.clip(1.0 + 0.18 * jax.random.normal(keys[1], (D,), jnp.float32), 0.1, 1.9),
        "gate_tiles": normal_values(keys[2], (N_TENSOR, N_DP, KCAP, TILE * TILE), (D // 2) ** -0.5, 0.125, ((0, 16), (1, 32))),
        "up_tiles": normal_values(keys[3], (N_TENSOR, N_DP, KCAP, TILE * TILE), (D // 2) ** -0.5, 0.125, ((0, 16), (1, 32))),
        "down_tiles": normal_values(keys[4], (N_TENSOR, N_DP, KCAP, TILE * TILE), (FF // 2) ** -0.5, 0.0625, ((0, 16), (1, 32))),
        "tile_ids": draw_tile_ids(jax.random.fold_in(keys[7], 71), 0),
        "tile_counts": draw_tile_counts(jax.random.fold_in(keys[7], 71), 0),
    }


def normalize(values, norm_gain):
    wide = values.astype(jnp.float32)
    meansq = lax.optimization_barrier(jnp.mean(wide * wide, axis=-1, keepdims=True))
    return (wide * lax.rsqrt(meansq + 1e-05) * norm_gain).astype(jnp.bfloat16)

def scatter_blocks(packed, slot_ids, counts, outward):
    active = (jnp.arange(KCAP)[None, :] < counts[:, None]).astype(jnp.float32)
    rows = (jnp.arange(N_DP)[:, None] * ROW_TILES + slot_ids // COL_TILES).astype(jnp.int32)
    cols = (slot_ids % COL_TILES).astype(jnp.int32)
    blocks = packed.astype(jnp.float32).reshape(N_DP, KCAP, TILE, TILE) * active[:, :, None, None]
    if outward:
        grid = jnp.zeros((COL_TILES, D // TILE, TILE, TILE), jnp.float32).at[cols, rows].add(blocks)
        return grid.transpose(0, 2, 1, 3).reshape(COL_TILES * TILE, D)
    grid = jnp.zeros((D // TILE, COL_TILES, TILE, TILE), jnp.float32).at[rows, cols].add(blocks)
    return grid.transpose(0, 2, 1, 3).reshape(D, COL_TILES * TILE)

def reference(tokens, norm_gain, gate_tiles, up_tiles, down_tiles, tile_ids, tile_counts):
    normed = normalize(tokens, norm_gain).astype(jnp.float32)

    def rank_step(summed, slices):
        gate_part, up_part, down_part, ids_part, count_part = slices
        w_gate = scatter_blocks(gate_part, ids_part[:, 0], count_part[:, 0], False)
        w_up = scatter_blocks(up_part, ids_part[:, 1], count_part[:, 1], False)
        w_down = scatter_blocks(down_part, ids_part[:, 2], count_part[:, 2], True)
        gate = jnp.dot(normed, w_gate, preferred_element_type=jnp.float32)
        upward = jnp.dot(normed, w_up, preferred_element_type=jnp.float32)
        hidden = (jax.nn.silu(gate) * upward).astype(jnp.bfloat16)
        partial_value = jnp.dot(hidden.astype(jnp.float32), w_down, preferred_element_type=jnp.float32).astype(jnp.bfloat16)
        return (summed + partial_value.astype(jnp.float32), None)
    start_sum = jnp.zeros((normed.shape[0], D), jnp.float32)
    summed, ignored = lax.scan(rank_step, start_sum, (gate_tiles, up_tiles, down_tiles, tile_ids, tile_counts))
    return summed.astype(jnp.bfloat16)
```

```python
import jax
import jax.numpy as jnp
from jax import lax
from jax.experimental import pallas as pl
from jax.experimental.pallas import tpu as pltpu
from jax.sharding import PartitionSpec as P

D = 4096
FF = 14336
TILE = 64
HALF = TILE // 2
LANES = 2 * TILE
META_ROWS = 16
IN_PEERS = 4
OUT_PEERS = 4


def normalize(values, norm_gain):
    wide = values.astype(jnp.float32)
    meansq = jnp.mean(wide * wide, axis=-1, keepdims=True)
    return (wide * lax.rsqrt(meansq + 1e-05) * norm_gain).astype(jnp.bfloat16)


def slot_table(tile_ids, tile_counts, local_tiles):
    slots = tile_ids.shape[-1]
    order = jnp.arange(slots, dtype=jnp.int32)
    kept = order[None, :] < tile_counts[:, None]
    hit = (tile_ids[:, None, :] == jnp.arange(local_tiles)[None, :, None]) & kept[:, None, :]
    slot = order[None, :] + slots * jnp.arange(3, dtype=jnp.int32)[:, None]
    empty = 3 * slots
    return empty + jnp.sum(jnp.where(hit, slot[:, None, :] - empty, 0), axis=-1)


def feed_forward(table_ref, tokens_ref, gathered_ref, out_ref, tiles_ref, inward_ref, gate_ref, up_ref, hidden_ref, outward_ref, sems, *, peers, slots, row_tiles, col_tiles):
    local_tiles = row_tiles * col_tiles
    body_rows = 3 * slots * HALF
    split = 2 * slots * HALF
    in_chunks = peers // IN_PEERS
    out_chunks = peers // OUT_PEERS
    in_rows = IN_PEERS * row_tiles * TILE

    def inward_copy(chunk):
        where = pl.ds(chunk * IN_PEERS, IN_PEERS)
        return pltpu.make_async_copy(
            gathered_ref.at[where, pl.ds(0, split)], tiles_ref.at[where, pl.ds(0, split)], sems.at[0, chunk]
        )

    def outward_copy(chunk):
        where = pl.ds(chunk * OUT_PEERS, OUT_PEERS)
        rest = pl.ds(split, body_rows - split)
        return pltpu.make_async_copy(gathered_ref.at[where, rest], tiles_ref.at[where, rest], sems.at[1, chunk])

    for chunk in range(in_chunks):
        inward_copy(chunk).start()
    for chunk in range(out_chunks):
        outward_copy(chunk).start()
    tiles_ref[:, body_rows:, :] = jnp.zeros((peers, HALF, LANES), jnp.bfloat16)
    left = lax.broadcasted_iota(jnp.int32, (HALF, LANES), 1) < TILE

    def pair(peer, first, second):
        def load(entry):
            row = pl.multiple_of(table_ref[peer, entry] * HALF, HALF)
            return tiles_ref[peer, pl.ds(row, HALF), :]

        one, two = load(first), load(second)
        even = jnp.where(left, one, pltpu.roll(two, TILE, 1))
        odd = jnp.where(left, pltpu.roll(one, TILE, 1), two)
        return even, odd

    def inward_chunk(chunk, carry):
        inward_copy(chunk).wait()
        for local_peer in range(IN_PEERS):
            peer = chunk * IN_PEERS + local_peer
            for matrix in range(2):
                for row in range(row_tiles):
                    for col in range(0, col_tiles, 2):
                        entry = matrix * local_tiles + row * col_tiles + col
                        even, odd = pair(peer, entry, entry + 1)
                        at = (local_peer * row_tiles + row) * TILE
                        lanes = slice(col * TILE, (col + 2) * TILE)
                        inward_ref[matrix, at : at + HALF, lanes] = even
                        inward_ref[matrix, at + HALF : at + TILE, lanes] = odd
        rows = tokens_ref[:, pl.ds(pl.multiple_of(chunk * in_rows, in_rows), in_rows)]
        gate_ref[...] += jnp.dot(rows, inward_ref[0], preferred_element_type=jnp.float32)
        up_ref[...] += jnp.dot(rows, inward_ref[1], preferred_element_type=jnp.float32)
        return carry

    gate_ref[...] = jnp.zeros_like(gate_ref)
    up_ref[...] = jnp.zeros_like(up_ref)
    lax.fori_loop(0, in_chunks, inward_chunk, 0)

    source = lax.broadcasted_iota(jnp.int32, (LANES, LANES), 0)
    target = lax.broadcasted_iota(jnp.int32, (LANES, LANES), 1)
    inner = target % TILE
    wanted = target - inner + jnp.where(inner < HALF, 2 * inner, 2 * (inner - HALF) + 1)
    shuffle = (source == wanted).astype(jnp.bfloat16)
    for block in range(col_tiles // 2):
        lanes = slice(block * LANES, (block + 1) * LANES)
        value = (jax.nn.silu(gate_ref[:, lanes]) * up_ref[:, lanes]).astype(jnp.bfloat16)
        hidden_ref[:, lanes] = jnp.dot(value, shuffle, preferred_element_type=jnp.float32).astype(jnp.bfloat16)

    out_lanes = OUT_PEERS * LANES

    def outward_chunk(chunk, carry):
        outward_copy(chunk).wait()
        for local_peer in range(OUT_PEERS):
            peer = chunk * OUT_PEERS + local_peer
            for col in range(col_tiles):
                entry = 2 * local_tiles + col
                even, odd = pair(peer, entry, entry + col_tiles)
                lanes = slice(local_peer * LANES, (local_peer + 1) * LANES)
                outward_ref[col * TILE : col * TILE + HALF, lanes] = even
                outward_ref[col * TILE + HALF : (col + 1) * TILE, lanes] = odd
        value = jnp.dot(hidden_ref[...], outward_ref[...], preferred_element_type=jnp.float32)
        out_ref[:, pl.ds(pl.multiple_of(chunk * out_lanes, out_lanes), out_lanes)] = value.astype(jnp.bfloat16)
        return carry

    lax.fori_loop(0, out_chunks, outward_chunk, 0)


def apply_tiles(table, rows, gathered, *, slots, row_tiles, col_tiles, interpret=False):
    import functools

    peers = gathered.shape[0]
    tokens, width = rows.shape
    hidden = col_tiles * TILE
    vmem = pl.BlockSpec(memory_space=pltpu.VMEM)
    return pl.pallas_call(
        functools.partial(feed_forward, peers=peers, slots=slots, row_tiles=row_tiles, col_tiles=col_tiles),
        out_shape=jax.ShapeDtypeStruct((tokens, width), jnp.bfloat16),
        in_specs=[pl.BlockSpec(memory_space=pltpu.SMEM), vmem, pl.BlockSpec(memory_space=pl.ANY)],
        out_specs=vmem,
        scratch_shapes=[
            pltpu.VMEM((peers, 3 * slots * HALF + HALF, LANES), jnp.bfloat16),
            pltpu.VMEM((2, IN_PEERS * row_tiles * TILE, hidden), jnp.bfloat16),
            pltpu.VMEM((tokens, hidden), jnp.float32),
            pltpu.VMEM((tokens, hidden), jnp.float32),
            pltpu.VMEM((tokens, hidden), jnp.bfloat16),
            pltpu.VMEM((hidden, OUT_PEERS * LANES), jnp.bfloat16),
            pltpu.SemaphoreType.DMA((2, max(peers // IN_PEERS, peers // OUT_PEERS))),
        ],
        compiler_params=pltpu.CompilerParams(vmem_limit_bytes=56 * 1024 * 1024),
        interpret=interpret,
        name="feed_forward",
    )(table, rows, gathered)


def pack(gate_tiles, up_tiles, down_tiles, tile_ids, tile_counts, local_tiles):
    tiles = jnp.concatenate([gate_tiles, up_tiles, down_tiles], axis=0)
    tiles = tiles.reshape(tiles.shape[0] * HALF, LANES)
    table = slot_table(tile_ids, tile_counts, local_tiles).astype(jnp.bfloat16)
    meta = jnp.pad(table, ((0, META_ROWS - 3), (0, LANES - local_tiles)))
    return jnp.concatenate([tiles, meta], axis=0)


def even_odd(values):
    rows, width = values.shape
    return values.reshape(rows, width // TILE, HALF, 2).swapaxes(2, 3).reshape(rows, width)


def local(tokens, norm_gain, gate_tiles, up_tiles, down_tiles, tile_ids, tile_counts):
    peers = lax.axis_size("dp")
    members = lax.axis_size("tensor")
    row_tiles = D // (TILE * peers)
    col_tiles = FF // (TILE * members)
    local_tiles = row_tiles * col_tiles
    slots = gate_tiles.shape[2]
    body_rows = 3 * slots * HALF
    packed = pack(gate_tiles[0, 0], up_tiles[0, 0], down_tiles[0, 0], tile_ids[0, 0], tile_counts[0, 0], local_tiles)
    gathered = lax.all_gather(packed, "dp", axis=0)
    mine = even_odd(normalize(tokens, norm_gain))
    copies = jnp.broadcast_to(mine[None], (members,) + mine.shape)
    group_rows = lax.all_to_all(copies, "tensor", 0, 0).reshape(members * mine.shape[0], D)
    table = gathered[:, body_rows : body_rows + 3, :local_tiles].astype(jnp.int32).reshape(peers, 3 * local_tiles)
    partial_value = apply_tiles(
        table, group_rows, gathered, slots=slots, row_tiles=row_tiles, col_tiles=col_tiles
    )
    terms = lax.all_to_all(partial_value.reshape(members, mine.shape[0], D), "tensor", 0, 0)
    return jnp.sum(terms.astype(jnp.float32), axis=0).astype(jnp.bfloat16)


def solution(mesh):
    return jax.shard_map(
        local,
        mesh=mesh,
        in_specs=(
            P(("dp", "tensor"), None),
            P(),
            P("tensor", "dp", None, None),
            P("tensor", "dp", None, None),
            P("tensor", "dp", None, None),
            P("tensor", "dp", None, None),
            P("tensor", "dp", None),
        ),
        out_specs=P(("dp", "tensor"), None),
        check_vma=False,
    )
```

```python
import jax
import jax.numpy as jnp
from jax import lax
from jax.experimental import pallas as pl
from jax.experimental.pallas import tpu as pltpu
from jax.sharding import PartitionSpec as P

D = 4096
FF = 14336
TILE = 64
HALF = TILE // 2
LANES = 2 * TILE
META_ROWS = 16
IN_PEERS = 4
OUT_PEERS = 4


def normalize(values, norm_gain):
    wide = values.astype(jnp.float32)
    meansq = jnp.mean(wide * wide, axis=-1, keepdims=True)
    return (wide * lax.rsqrt(meansq + 1e-05) * norm_gain).astype(jnp.bfloat16)


def slot_table(tile_ids, tile_counts, local_tiles):
    slots = tile_ids.shape[-1]
    order = jnp.arange(slots, dtype=jnp.int32)
    kept = order[None, :] < tile_counts[:, None]
    hit = (tile_ids[:, None, :] == jnp.arange(local_tiles)[None, :, None]) & kept[:, None, :]
    slot = order[None, :] + slots * jnp.arange(3, dtype=jnp.int32)[:, None]
    empty = 3 * slots
    return empty + jnp.sum(jnp.where(hit, slot[:, None, :] - empty, 0), axis=-1)


def feed_forward(table_ref, tokens_ref, gathered_ref, out_ref, tiles_ref, inward_ref, gate_ref, up_ref, hidden_ref, outward_ref, sems, *, peers, slots, row_tiles, col_tiles):
    local_tiles = row_tiles * col_tiles
    body_rows = 3 * slots * HALF
    split = 2 * slots * HALF
    in_chunks = peers // IN_PEERS
    out_chunks = peers // OUT_PEERS
    in_rows = IN_PEERS * row_tiles * TILE

    def inward_copy(chunk):
        where = pl.ds(chunk * IN_PEERS, IN_PEERS)
        return pltpu.make_async_copy(
            gathered_ref.at[where, pl.ds(0, split)], tiles_ref.at[where, pl.ds(0, split)], sems.at[0, chunk]
        )

    def outward_copy(chunk):
        where = pl.ds(chunk * OUT_PEERS, OUT_PEERS)
        rest = pl.ds(split, body_rows - split)
        return pltpu.make_async_copy(gathered_ref.at[where, rest], tiles_ref.at[where, rest], sems.at[1, chunk])

    for chunk in range(in_chunks):
        inward_copy(chunk).start()
    for chunk in range(out_chunks):
        outward_copy(chunk).start()
    tiles_ref[:, body_rows:, :] = jnp.zeros((peers, HALF, LANES), jnp.bfloat16)
    left = lax.broadcasted_iota(jnp.int32, (HALF, LANES), 1) < TILE

    def pair(peer, first, second):
        def load(entry):
            row = pl.multiple_of(table_ref[peer, entry // local_tiles, entry % local_tiles] * HALF, HALF)
            return tiles_ref[peer, pl.ds(row, HALF), :]

        one, two = load(first), load(second)
        even = jnp.where(left, one, pltpu.roll(two, TILE, 1))
        odd = jnp.where(left, pltpu.roll(one, TILE, 1), two)
        return even, odd

    def inward_chunk(chunk, carry):
        inward_copy(chunk).wait()
        for local_peer in range(IN_PEERS):
            peer = chunk * IN_PEERS + local_peer
            for matrix in range(2):
                for row in range(row_tiles):
                    for col in range(0, col_tiles, 2):
                        entry = matrix * local_tiles + row * col_tiles + col
                        even, odd = pair(peer, entry, entry + 1)
                        at = (local_peer * row_tiles + row) * TILE
                        lanes = slice(col * TILE, (col + 2) * TILE)
                        inward_ref[matrix, at : at + HALF, lanes] = even
                        inward_ref[matrix, at + HALF : at + TILE, lanes] = odd
        rows = tokens_ref[:, pl.ds(pl.multiple_of(chunk * in_rows, in_rows), in_rows)]
        gate_ref[...] += jnp.dot(rows, inward_ref[0], preferred_element_type=jnp.float32)
        up_ref[...] += jnp.dot(rows, inward_ref[1], preferred_element_type=jnp.float32)
        return carry

    gate_ref[...] = jnp.zeros_like(gate_ref)
    up_ref[...] = jnp.zeros_like(up_ref)
    lax.fori_loop(0, in_chunks, inward_chunk, 0)

    source = lax.broadcasted_iota(jnp.int32, (LANES, LANES), 0)
    target = lax.broadcasted_iota(jnp.int32, (LANES, LANES), 1)
    inner = target % TILE
    wanted = target - inner + jnp.where(inner < HALF, 2 * inner, 2 * (inner - HALF) + 1)
    shuffle = (source == wanted).astype(jnp.bfloat16)
    for block in range(col_tiles // 2):
        lanes = slice(block * LANES, (block + 1) * LANES)
        value = (jax.nn.silu(gate_ref[:, lanes]) * up_ref[:, lanes]).astype(jnp.bfloat16)
        hidden_ref[:, lanes] = jnp.dot(value, shuffle, preferred_element_type=jnp.float32).astype(jnp.bfloat16)

    out_lanes = OUT_PEERS * LANES

    def outward_chunk(chunk, carry):
        outward_copy(chunk).wait()
        for local_peer in range(OUT_PEERS):
            peer = chunk * OUT_PEERS + local_peer
            for col in range(col_tiles):
                entry = 2 * local_tiles + col
                even, odd = pair(peer, entry, entry + col_tiles)
                lanes = slice(local_peer * LANES, (local_peer + 1) * LANES)
                outward_ref[col * TILE : col * TILE + HALF, lanes] = even
                outward_ref[col * TILE + HALF : (col + 1) * TILE, lanes] = odd
        value = jnp.dot(hidden_ref[...], outward_ref[...], preferred_element_type=jnp.float32)
        out_ref[:, pl.ds(pl.multiple_of(chunk * out_lanes, out_lanes), out_lanes)] = value.astype(jnp.bfloat16)
        return carry

    lax.fori_loop(0, out_chunks, outward_chunk, 0)


def apply_tiles(table, rows, gathered, *, slots, row_tiles, col_tiles, interpret=False):
    import functools

    peers = gathered.shape[0]
    tokens, width = rows.shape
    hidden = col_tiles * TILE
    vmem = pl.BlockSpec(memory_space=pltpu.VMEM)
    return pl.pallas_call(
        functools.partial(feed_forward, peers=peers, slots=slots, row_tiles=row_tiles, col_tiles=col_tiles),
        out_shape=jax.ShapeDtypeStruct((tokens, width), jnp.bfloat16),
        in_specs=[pl.BlockSpec(memory_space=pltpu.SMEM), vmem, pl.BlockSpec(memory_space=pl.ANY)],
        out_specs=vmem,
        scratch_shapes=[
            pltpu.VMEM((peers, 3 * slots * HALF + HALF, LANES), jnp.bfloat16),
            pltpu.VMEM((2, IN_PEERS * row_tiles * TILE, hidden), jnp.bfloat16),
            pltpu.VMEM((tokens, hidden), jnp.float32),
            pltpu.VMEM((tokens, hidden), jnp.float32),
            pltpu.VMEM((tokens, hidden), jnp.bfloat16),
            pltpu.VMEM((hidden, OUT_PEERS * LANES), jnp.bfloat16),
            pltpu.SemaphoreType.DMA((2, max(peers // IN_PEERS, peers // OUT_PEERS))),
        ],
        compiler_params=pltpu.CompilerParams(vmem_limit_bytes=56 * 1024 * 1024),
        interpret=interpret,
        name="feed_forward",
    )(table, rows, gathered)


def pack(gate_tiles, up_tiles, down_tiles, tile_ids, tile_counts, local_tiles):
    tiles = jnp.concatenate([gate_tiles, up_tiles, down_tiles], axis=0)
    tiles = tiles.reshape(tiles.shape[0] * HALF, LANES)
    table = slot_table(tile_ids, tile_counts, local_tiles).astype(jnp.bfloat16)
    meta = jnp.pad(table, ((0, META_ROWS - 3), (0, LANES - local_tiles)))
    return jnp.concatenate([tiles, meta], axis=0)


def even_odd(values):
    rows, width = values.shape
    return values.reshape(rows, width // TILE, HALF, 2).swapaxes(2, 3).reshape(rows, width)


def group_side(members):
    side = 1
    while side * side < members:
        side *= 2
    return side


def gather_rows(values, groups):
    copies = jnp.broadcast_to(values[None], (len(groups[0]),) + values.shape)
    return lax.all_to_all(copies, "tensor", 0, 0, axis_index_groups=groups)


def reduce_rows(terms, groups):
    terms = lax.all_to_all(terms, "tensor", 0, 0, axis_index_groups=groups)
    return jnp.sum(terms.astype(jnp.float32), axis=0).astype(jnp.bfloat16)


def local(tokens, norm_gain, gate_tiles, up_tiles, down_tiles, tile_ids, tile_counts):
    peers = lax.axis_size("dp")
    members = lax.axis_size("tensor")
    row_tiles = D // (TILE * peers)
    col_tiles = FF // (TILE * members)
    local_tiles = row_tiles * col_tiles
    slots = gate_tiles.shape[2]
    body_rows = 3 * slots * HALF
    packed = pack(gate_tiles[0, 0], up_tiles[0, 0], down_tiles[0, 0], tile_ids[0, 0], tile_counts[0, 0], local_tiles)
    gathered = lax.all_gather(packed, "dp", axis=0)
    mine = even_odd(normalize(tokens, norm_gain))
    rows = mine.shape[0]
    across = group_side(members)
    along = members // across
    x_groups = [[y * across + x for x in range(across)] for y in range(along)]
    y_groups = [[y * across + x for y in range(along)] for x in range(across)]
    group_rows = gather_rows(mine, y_groups)
    group_rows = gather_rows(group_rows.reshape(along * rows, D), x_groups).reshape(members * rows, D)
    table = gathered[:, body_rows : body_rows + 3, :local_tiles].astype(jnp.int32)
    partial_value = apply_tiles(
        table, group_rows, gathered, slots=slots, row_tiles=row_tiles, col_tiles=col_tiles
    )
    summed = reduce_rows(partial_value.reshape(across, along * rows, D), x_groups)
    return reduce_rows(summed.reshape(along, rows, D), y_groups)


def solution(mesh):
    return jax.shard_map(
        local,
        mesh=mesh,
        in_specs=(
            P(("dp", "tensor"), None),
            P(),
            P("tensor", "dp", None, None),
            P("tensor", "dp", None, None),
            P("tensor", "dp", None, None),
            P("tensor", "dp", None, None),
            P("tensor", "dp", None),
        ),
        out_specs=P(("dp", "tensor"), None),
        check_vma=False,
    )
```

```python
import functools

import jax
import jax.numpy as jnp
from jax import lax
from jax.experimental import pallas as pl
from jax.experimental.pallas import tpu as pltpu
from jax.sharding import PartitionSpec as P

D = 4096
FF = 14336
TILE = 64
HALF = TILE // 2
LANES = 2 * TILE
IN_PEERS = 4
OUT_PEERS = 4
ORDER = (0, 3, 1, 2)
BLOCKS = (((0, 1), (2, 3)), ((0, 2), (1, 3)))


def normalize(values, norm_gain):
    wide = values.astype(jnp.float32)
    meansq = jnp.mean(wide * wide, axis=-1, keepdims=True)
    return (wide * lax.rsqrt(meansq + 1e-05) * norm_gain).astype(jnp.bfloat16)


def slot_table(tile_ids, tile_counts, local_tiles):
    slots = tile_ids.shape[-1]
    order = jnp.arange(slots, dtype=jnp.int32)
    kept = order[None, :] < tile_counts[:, None]
    hit = (tile_ids[:, None, :] == jnp.arange(local_tiles)[None, :, None]) & kept[:, None, :]
    matrix = jnp.arange(3, dtype=jnp.int32)[:, None]
    slot = order[None, :] + slots * (matrix == 1)
    empty = jnp.where(matrix == 2, slots, 2 * slots)
    return empty + jnp.sum(jnp.where(hit, (slot - empty)[:, None, :], 0), axis=-1)


def zero_rows(tiles_ref, rows):
    peers = tiles_ref.shape[0]
    tiles_ref[:, rows:, :] = jnp.zeros((peers, HALF, LANES), jnp.bfloat16)


def place(tiles_ref, peer, first, second):
    left = lax.broadcasted_iota(jnp.int32, (HALF, LANES), 1) < TILE

    def load(slot):
        return tiles_ref[peer, pl.ds(pl.multiple_of(slot * HALF, HALF), HALF), :]

    one, two = load(first), load(second)
    even = jnp.where(left, one, pltpu.roll(two, TILE, 1))
    odd = jnp.where(left, pltpu.roll(one, TILE, 1), two)
    return even, odd


def copy_chunk(gathered_ref, tiles_ref, sem_ref, chunk, size, first_peer, first_row, rows):
    source = gathered_ref.at[pl.ds(first_peer + chunk * size, size), pl.ds(first_row, rows)]
    return pltpu.make_async_copy(source, tiles_ref.at[pl.ds(chunk * size, size), pl.ds(0, rows)], sem_ref.at[chunk])


def outward_part(table_ref, hidden_ref, tiles_ref, outward_ref, out_refs, copy, *, blocks, first_peer, peers, local_tiles, col_tiles):
    out_lanes = OUT_PEERS * LANES

    def outward_chunk(chunk, carry):
        copy(chunk).wait()
        for local_peer in range(OUT_PEERS):
            peer = chunk * OUT_PEERS + local_peer
            for col in range(col_tiles):
                entry = 2 * local_tiles + col
                first = table_ref[first_peer + peer, entry]
                second = table_ref[first_peer + peer, entry + col_tiles]
                even, odd = place(tiles_ref, peer, first, second)
                lanes = slice(local_peer * LANES, (local_peer + 1) * LANES)
                outward_ref[col * TILE : col * TILE + HALF, lanes] = even
                outward_ref[col * TILE + HALF : (col + 1) * TILE, lanes] = odd
        value = jnp.dot(hidden_ref[...], outward_ref[...], preferred_element_type=jnp.float32)
        value = value.astype(jnp.bfloat16)
        size = value.shape[0] // len(ORDER)
        at = pl.ds(pl.multiple_of(chunk * out_lanes, out_lanes), out_lanes)
        for out_ref, chosen in zip(out_refs, blocks):
            for position, block in enumerate(chosen):
                out_ref[position * size : (position + 1) * size, at] = value[block * size : (block + 1) * size]
        return carry

    lax.fori_loop(0, peers // OUT_PEERS, outward_chunk, 0)


def inward_kernel(table_ref, order_ref, tokens_ref, gathered_ref, hidden_ref, keep_ref, send_ref, rows_ref, tiles_ref, down_ref, inward_ref, gate_ref, up_ref, outward_ref, token_sems, in_sems, out_sems, *, blocks, peers, out_peers, slots, row_tiles, col_tiles):
    local_tiles = row_tiles * col_tiles
    in_rows = IN_PEERS * row_tiles * TILE
    split = 2 * slots * HALF
    down_rows = slots * HALF

    members = token_sems.shape[0]
    size = rows_ref.shape[0] // members

    def token_copy(block):
        source = pl.ds(pl.multiple_of(order_ref[0, block] * size, size), size)
        return pltpu.make_async_copy(tokens_ref.at[source], rows_ref.at[pl.ds(block * size, size)], token_sems.at[block])

    def inward_copy(chunk):
        return copy_chunk(gathered_ref, tiles_ref, in_sems, chunk, IN_PEERS, 0, 0, split)

    def outward_copy(chunk):
        return copy_chunk(gathered_ref, down_ref, out_sems, chunk, OUT_PEERS, 0, split, down_rows)

    inward_copy(0).start()
    for block in range(members):
        token_copy(block).start()
    for chunk in range(1, peers // IN_PEERS):
        inward_copy(chunk).start()
    for chunk in range(out_peers // OUT_PEERS):
        outward_copy(chunk).start()
    zero_rows(tiles_ref, split)
    zero_rows(down_ref, down_rows)
    gate_ref[...] = jnp.zeros_like(gate_ref)
    up_ref[...] = jnp.zeros_like(up_ref)
    for block in range(members):
        token_copy(block).wait()

    def inward_chunk(chunk, carry):
        inward_copy(chunk).wait()
        for local_peer in range(IN_PEERS):
            peer = chunk * IN_PEERS + local_peer
            for matrix in range(2):
                for row in range(row_tiles):
                    for col in range(0, col_tiles, 2):
                        entry = matrix * local_tiles + row * col_tiles + col
                        even, odd = place(tiles_ref, peer, table_ref[peer, entry], table_ref[peer, entry + 1])
                        at = (local_peer * row_tiles + row) * TILE
                        lanes = slice(col * TILE, (col + 2) * TILE)
                        inward_ref[matrix, at : at + HALF, lanes] = even
                        inward_ref[matrix, at + HALF : at + TILE, lanes] = odd
        rows = rows_ref[:, pl.ds(pl.multiple_of(chunk * in_rows, in_rows), in_rows)]
        gate_ref[...] += jnp.dot(rows, inward_ref[0], preferred_element_type=jnp.float32)
        up_ref[...] += jnp.dot(rows, inward_ref[1], preferred_element_type=jnp.float32)
        return carry

    lax.fori_loop(0, peers // IN_PEERS, inward_chunk, 0)

    source = lax.broadcasted_iota(jnp.int32, (LANES, LANES), 0)
    target = lax.broadcasted_iota(jnp.int32, (LANES, LANES), 1)
    inner = target % TILE
    wanted = target - inner + jnp.where(inner < HALF, 2 * inner, 2 * (inner - HALF) + 1)
    shuffle = (source == wanted).astype(jnp.bfloat16)
    for block in range(col_tiles // 2):
        lanes = slice(block * LANES, (block + 1) * LANES)
        value = (jax.nn.silu(gate_ref[:, lanes]) * up_ref[:, lanes]).astype(jnp.bfloat16)
        hidden_ref[:, lanes] = jnp.dot(value, shuffle, preferred_element_type=jnp.float32).astype(jnp.bfloat16)

    outward_part(
        table_ref, hidden_ref, down_ref, outward_ref, (keep_ref, send_ref), outward_copy, blocks=blocks, first_peer=0, peers=out_peers, local_tiles=local_tiles, col_tiles=col_tiles
    )


def outward_kernel(table_ref, hidden_ref, gathered_ref, keep_ref, send_ref, down_ref, outward_ref, out_sems, *, blocks, first_peer, out_peers, slots, row_tiles, col_tiles):
    local_tiles = row_tiles * col_tiles
    split = 2 * slots * HALF
    down_rows = slots * HALF

    def outward_copy(chunk):
        return copy_chunk(gathered_ref, down_ref, out_sems, chunk, OUT_PEERS, first_peer, split, down_rows)

    for chunk in range(out_peers // OUT_PEERS):
        outward_copy(chunk).start()
    zero_rows(down_ref, down_rows)
    outward_part(
        table_ref, hidden_ref, down_ref, outward_ref, (keep_ref, send_ref), outward_copy, blocks=blocks, first_peer=first_peer, peers=out_peers, local_tiles=local_tiles, col_tiles=col_tiles
    )


SMEM = pl.BlockSpec(memory_space=pltpu.SMEM)
VMEM = pl.BlockSpec(memory_space=pltpu.VMEM)
ANY = pl.BlockSpec(memory_space=pl.ANY)
PARAMS = pltpu.CompilerParams(vmem_limit_bytes=56 * 1024 * 1024)


def down_scratch(out_peers, slots, hidden):
    return [
        pltpu.VMEM((out_peers, slots * HALF + HALF, LANES), jnp.bfloat16),
        pltpu.VMEM((hidden, OUT_PEERS * LANES), jnp.bfloat16),
        pltpu.SemaphoreType.DMA((out_peers // OUT_PEERS,)),
    ]


def halves(tokens, out_peers):
    shape = jax.ShapeDtypeStruct((tokens // 2, out_peers * LANES), jnp.bfloat16)
    return (shape, shape)


def apply_inward(table, order, rows, gathered, out_peers, blocks, *, slots, row_tiles, col_tiles, interpret=False):
    peers = gathered.shape[0]
    tokens, width = rows.shape
    hidden = col_tiles * TILE
    down, outward, out_sems = down_scratch(out_peers, slots, hidden)
    body = functools.partial(
        inward_kernel, blocks=blocks, peers=peers, out_peers=out_peers, slots=slots, row_tiles=row_tiles, col_tiles=col_tiles
    )
    return pl.pallas_call(
        body,
        out_shape=(
            jax.ShapeDtypeStruct((tokens, hidden), jnp.bfloat16),
            *halves(tokens, out_peers),
        ),
        in_specs=[SMEM, SMEM, ANY, ANY],
        out_specs=(VMEM, VMEM, VMEM),
        scratch_shapes=[
            pltpu.VMEM((tokens, width), jnp.bfloat16),
            pltpu.VMEM((peers, 2 * slots * HALF + HALF, LANES), jnp.bfloat16),
            down,
            pltpu.VMEM((2, IN_PEERS * row_tiles * TILE, hidden), jnp.bfloat16),
            pltpu.VMEM((tokens, hidden), jnp.float32),
            pltpu.VMEM((tokens, hidden), jnp.float32),
            outward,
            pltpu.SemaphoreType.DMA((order.shape[1],)),
            pltpu.SemaphoreType.DMA((peers // IN_PEERS,)),
            out_sems,
        ],
        compiler_params=PARAMS,
        interpret=interpret,
        name="inward",
    )(table, order, rows, gathered)


def apply_outward(table, hidden, gathered, first_peer, out_peers, blocks, *, slots, row_tiles, col_tiles, interpret=False):
    body = functools.partial(
        outward_kernel, blocks=blocks, first_peer=first_peer, out_peers=out_peers, slots=slots, row_tiles=row_tiles, col_tiles=col_tiles
    )
    return pl.pallas_call(
        body,
        out_shape=halves(hidden.shape[0], out_peers),
        in_specs=[SMEM, VMEM, ANY],
        out_specs=(VMEM, VMEM),
        scratch_shapes=down_scratch(out_peers, slots, hidden.shape[1]),
        compiler_params=PARAMS,
        interpret=interpret,
        name="outward",
    )(table, hidden, gathered)


def even_odd(values):
    rows, width = values.shape
    return values.reshape(rows, width // TILE, HALF, 2).swapaxes(2, 3).reshape(rows, width)


def group_side(members):
    side = 1
    while side * side < members:
        side *= 2
    return side


def gather_rows(values, groups):
    copies = jnp.broadcast_to(values[None], (len(groups[0]),) + values.shape)
    return lax.all_to_all(copies, "tensor", 0, 0, axis_index_groups=groups)


def exchange(keep, send, step, members):
    got = lax.ppermute(send, "tensor", [(t, t ^ step) for t in range(members)])
    return (keep.astype(jnp.float32) + got.astype(jnp.float32)).astype(jnp.bfloat16)


def reduce_stream(keep, send, blocks, steps, across, members):
    first, second = steps
    value = exchange(keep, send, first, members)
    half = value.shape[0] // 2
    value = exchange(value[:half], value[half:], second, members)
    size = value.shape[0] // len(ORDER)
    keep, send = (
        jnp.concatenate([value[block * size : (block + 1) * size] for block in chosen]) for chosen in blocks
    )
    value = exchange(keep, send, first * across, members)
    half = value.shape[0] // 2
    return exchange(value[:half], value[half:], second * across, members)


def local(tokens, norm_gain, gate_tiles, up_tiles, down_tiles, tile_ids, tile_counts):
    peers = lax.axis_size("dp")
    members = lax.axis_size("tensor")
    row_tiles = D // (TILE * peers)
    col_tiles = FF // (TILE * members)
    local_tiles = row_tiles * col_tiles
    slots = gate_tiles.shape[2]
    tiles = jnp.concatenate([gate_tiles[0, 0], up_tiles[0, 0], down_tiles[0, 0]], axis=0)
    gathered = lax.all_gather(tiles.reshape(3 * slots * HALF, LANES), "dp", axis=0)
    mine = even_odd(normalize(tokens, norm_gain))
    rows = mine.shape[0]
    across = group_side(members)
    along = members // across
    x_groups = [[y * across + x for x in range(across)] for y in range(along)]
    y_groups = [[y * across + x for y in range(along)] for x in range(across)]
    group_rows = gather_rows(mine, y_groups)
    entry = slot_table(tile_ids[0, 0], tile_counts[0, 0], local_tiles).reshape(1, 3 * local_tiles)
    entry = jnp.pad(entry, ((0, 0), (0, -entry.shape[1] % LANES)))
    entry, group_rows = lax.optimization_barrier((entry, group_rows))
    group_rows = gather_rows(group_rows.reshape(along * rows, D), x_groups).reshape(members * rows, D)
    table = lax.all_gather(entry, "dp", axis=0, tiled=True)
    assert across == along == len(ORDER)
    place_x, place_y = lax.axis_index("tensor") % across, lax.axis_index("tensor") // across
    offsets = jnp.asarray(ORDER, jnp.int32)
    order = (place_x ^ offsets)[:, None] * along + (place_y ^ offsets)[None, :]
    order = order.astype(jnp.int32).reshape(1, members)
    sizes = dict(slots=slots, row_tiles=row_tiles, col_tiles=col_tiles)
    early = peers // 2
    hidden, keep, send = apply_inward(table, order, group_rows, gathered, early, BLOCKS[0], **sizes)
    first = reduce_stream(keep, send, BLOCKS[0], (1, 3), across, members)
    keep, send = apply_outward(table, hidden, gathered, early, peers - early, BLOCKS[1], **sizes)
    second = reduce_stream(keep, send, BLOCKS[1], (3, 1), across, members)
    return jnp.concatenate([first, second], axis=1)


def solution(mesh):
    return jax.shard_map(
        local,
        mesh=mesh,
        in_specs=(
            P(("dp", "tensor"), None),
            P(),
            P("tensor", "dp", None, None),
            P("tensor", "dp", None, None),
            P("tensor", "dp", None, None),
            P("tensor", "dp", None, None),
            P("tensor", "dp", None),
        ),
        out_specs=P(("dp", "tensor"), None),
        check_vma=False,
    )
```

```python
import functools

import jax
import jax.numpy as jnp
from jax import lax
from jax.experimental import pallas as pl
from jax.experimental.pallas import tpu as pltpu
from jax.sharding import PartitionSpec as P

D = 4096
FF = 14336
TILE = 64
HALF = TILE // 2
LANES = 2 * TILE
IN_PEERS = 4
OUT_PEERS = 4
ORDER = (0, 3, 1, 2)
BLOCKS = (((0, 1), (2, 3)), ((0, 2), (1, 3)))


def normalize(values, norm_gain):
    wide = values.astype(jnp.float32)
    meansq = jnp.mean(wide * wide, axis=-1, keepdims=True)
    return (wide * lax.rsqrt(meansq + 1e-05) * norm_gain).astype(jnp.bfloat16)


def slot_table(tile_ids, tile_counts, local_tiles):
    slots = tile_ids.shape[-1]
    order = jnp.arange(slots, dtype=jnp.int32)
    kept = order[None, :] < tile_counts[:, None]
    hit = (tile_ids[:, None, :] == jnp.arange(local_tiles)[None, :, None]) & kept[:, None, :]
    matrix = jnp.arange(3, dtype=jnp.int32)[:, None]
    slot = order[None, :] + slots * (matrix == 1)
    empty = jnp.where(matrix == 2, slots, 2 * slots)
    return empty + jnp.sum(jnp.where(hit, (slot - empty)[:, None, :], 0), axis=-1)


def zero_rows(tiles_ref, rows):
    peers = tiles_ref.shape[0]
    tiles_ref[:, rows:, :] = jnp.zeros((peers, HALF, LANES), jnp.bfloat16)


def place(tiles_ref, peer, first, second):
    left = lax.broadcasted_iota(jnp.int32, (HALF, LANES), 1) < TILE

    def load(slot):
        return tiles_ref[peer, pl.ds(pl.multiple_of(slot * HALF, HALF), HALF), :]

    one, two = load(first), load(second)
    even = jnp.where(left, one, pltpu.roll(two, TILE, 1))
    odd = jnp.where(left, pltpu.roll(one, TILE, 1), two)
    return even, odd


def copy_chunk(gathered_ref, tiles_ref, sem_ref, chunk, size, first_row, rows):
    source = gathered_ref.at[pl.ds(chunk * size, size), pl.ds(first_row, rows)]
    return pltpu.make_async_copy(source, tiles_ref.at[pl.ds(chunk * size, size), pl.ds(0, rows)], sem_ref.at[chunk])


def feed_forward(table_ref, order_ref, tokens_ref, gathered_ref, *refs, peers, slots, row_tiles, col_tiles):
    out_refs, refs = refs[:4], refs[4:]
    rows_ref, tiles_ref, down_ref, gate_ref, up_ref, hidden_ref = refs[:6]
    inward_refs, outward_refs, token_sems, in_sems, out_sems = refs[6:8], refs[8:10], *refs[10:]
    local_tiles = row_tiles * col_tiles
    in_chunks = peers // IN_PEERS
    out_chunks = peers // OUT_PEERS
    in_rows = IN_PEERS * row_tiles * TILE
    out_lanes = OUT_PEERS * LANES
    split = 2 * slots * HALF
    down_rows = slots * HALF
    members = token_sems.shape[0]
    size = rows_ref.shape[0] // members

    def token_copy(block):
        source = pl.ds(pl.multiple_of(order_ref[0, block] * size, size), size)
        return pltpu.make_async_copy(tokens_ref.at[source], rows_ref.at[pl.ds(block * size, size)], token_sems.at[block])

    def inward_copy(chunk):
        return copy_chunk(gathered_ref, tiles_ref, in_sems, chunk, IN_PEERS, 0, split)

    def outward_copy(chunk):
        return copy_chunk(gathered_ref, down_ref, out_sems, chunk, OUT_PEERS, split, down_rows)

    def inward_place(chunk, buffer):
        for local_peer in range(IN_PEERS):
            peer = chunk * IN_PEERS + local_peer
            for matrix in range(2):
                for row in range(row_tiles):
                    for col in range(0, col_tiles, 2):
                        entry = matrix * local_tiles + row * col_tiles + col
                        even, odd = place(tiles_ref, peer, table_ref[peer, entry], table_ref[peer, entry + 1])
                        at = (local_peer * row_tiles + row) * TILE
                        lanes = slice(col * TILE, (col + 2) * TILE)
                        buffer[matrix, at : at + HALF, lanes] = even
                        buffer[matrix, at + HALF : at + TILE, lanes] = odd

    def inward_multiply(chunk, buffer):
        rows = rows_ref[:, pl.ds(pl.multiple_of(chunk * in_rows, in_rows), in_rows)]
        gate_ref[...] += jnp.dot(rows, buffer[0], preferred_element_type=jnp.float32)
        up_ref[...] += jnp.dot(rows, buffer[1], preferred_element_type=jnp.float32)

    def outward_place(chunk, buffer):
        for local_peer in range(OUT_PEERS):
            peer = chunk * OUT_PEERS + local_peer
            for col in range(col_tiles):
                entry = 2 * local_tiles + col
                even, odd = place(down_ref, peer, table_ref[peer, entry], table_ref[peer, entry + col_tiles])
                lanes = slice(local_peer * LANES, (local_peer + 1) * LANES)
                buffer[col * TILE : col * TILE + HALF, lanes] = even
                buffer[col * TILE + HALF : (col + 1) * TILE, lanes] = odd

    def outward_multiply(chunk, lane_chunk, buffer, keep_ref, send_ref, blocks):
        value = jnp.dot(hidden_ref[...], buffer[...], preferred_element_type=jnp.float32).astype(jnp.bfloat16)
        part = value.shape[0] // len(ORDER)
        at = pl.ds(pl.multiple_of(lane_chunk * out_lanes, out_lanes), out_lanes)
        for out_ref, chosen in zip((keep_ref, send_ref), blocks):
            for position, block in enumerate(chosen):
                out_ref[position * part : (position + 1) * part, at] = value[block * part : (block + 1) * part]

    inward_copy(0).start()
    for block in range(members):
        token_copy(block).start()
    inward_copy(1).start()
    zero_rows(tiles_ref, split)
    zero_rows(down_ref, down_rows)
    gate_ref[...] = jnp.zeros_like(gate_ref)
    up_ref[...] = jnp.zeros_like(up_ref)
    inward_copy(0).wait()
    inward_place(0, inward_refs[0])
    for block in range(members):
        token_copy(block).wait()

    def inward_pair(pair, carry):
        chunk = 2 * pair

        @pl.when(chunk + 2 < in_chunks)
        def start_next():
            inward_copy(chunk + 2).start()
            inward_copy(chunk + 3).start()

        inward_copy(chunk + 1).wait()
        inward_place(chunk + 1, inward_refs[1])
        inward_multiply(chunk, inward_refs[0])

        @pl.when(chunk + 2 < in_chunks)
        def wait_next():
            inward_copy(chunk + 2).wait()

        @pl.when(chunk + 2 >= in_chunks)
        def start_outward():
            for later in range(out_chunks):
                outward_copy(later).start()

        inward_place(jnp.minimum(chunk + 2, in_chunks - 1), inward_refs[0])
        inward_multiply(chunk + 1, inward_refs[1])
        return carry

    lax.fori_loop(0, in_chunks // 2, inward_pair, 0)

    source = lax.broadcasted_iota(jnp.int32, (LANES, LANES), 0)
    target = lax.broadcasted_iota(jnp.int32, (LANES, LANES), 1)
    inner = target % TILE
    wanted = target - inner + jnp.where(inner < HALF, 2 * inner, 2 * (inner - HALF) + 1)
    shuffle = (source == wanted).astype(jnp.bfloat16)
    outward_copy(0).wait()
    outward_place(0, outward_refs[0])
    for block in range(col_tiles // 2):
        lanes = slice(block * LANES, (block + 1) * LANES)
        value = (jax.nn.silu(gate_ref[:, lanes]) * up_ref[:, lanes]).astype(jnp.bfloat16)
        hidden_ref[:, lanes] = jnp.dot(value, shuffle, preferred_element_type=jnp.float32).astype(jnp.bfloat16)

    half = out_chunks // 2
    for stream in range(2):
        targets = (out_refs[2 * stream], out_refs[2 * stream + 1], BLOCKS[stream])

        def outward_pair(pair, carry):
            chunk = stream * half + 2 * pair
            outward_copy(chunk + 1).wait()
            outward_place(chunk + 1, outward_refs[1])
            outward_multiply(chunk, 2 * pair, outward_refs[0], *targets)

            @pl.when(chunk + 2 < out_chunks)
            def wait_next():
                outward_copy(chunk + 2).wait()

            outward_place(jnp.minimum(chunk + 2, out_chunks - 1), outward_refs[0])
            outward_multiply(chunk + 1, 2 * pair + 1, outward_refs[1], *targets)
            return carry

        lax.fori_loop(0, half // 2, outward_pair, 0)


SMEM = pl.BlockSpec(memory_space=pltpu.SMEM)
VMEM = pl.BlockSpec(memory_space=pltpu.VMEM)
ANY = pl.BlockSpec(memory_space=pl.ANY)


def apply_tiles(table, order, rows, gathered, *, slots, row_tiles, col_tiles, interpret=False):
    peers = gathered.shape[0]
    tokens, width = rows.shape
    hidden = col_tiles * TILE
    part = jax.ShapeDtypeStruct((tokens // 2, width // 2), jnp.bfloat16)
    inward = pltpu.VMEM((2, IN_PEERS * row_tiles * TILE, hidden), jnp.bfloat16)
    outward = pltpu.VMEM((hidden, OUT_PEERS * LANES), jnp.bfloat16)
    return pl.pallas_call(
        functools.partial(feed_forward, peers=peers, slots=slots, row_tiles=row_tiles, col_tiles=col_tiles),
        out_shape=(part,) * 4,
        in_specs=[SMEM, SMEM, ANY, ANY],
        out_specs=(VMEM,) * 4,
        scratch_shapes=[
            pltpu.VMEM((tokens, width), jnp.bfloat16),
            pltpu.VMEM((peers, 2 * slots * HALF + HALF, LANES), jnp.bfloat16),
            pltpu.VMEM((peers, slots * HALF + HALF, LANES), jnp.bfloat16),
            pltpu.VMEM((tokens, hidden), jnp.float32),
            pltpu.VMEM((tokens, hidden), jnp.float32),
            pltpu.VMEM((tokens, hidden), jnp.bfloat16),
            inward,
            inward,
            outward,
            outward,
            pltpu.SemaphoreType.DMA((order.shape[1],)),
            pltpu.SemaphoreType.DMA((peers // IN_PEERS,)),
            pltpu.SemaphoreType.DMA((peers // OUT_PEERS,)),
        ],
        compiler_params=pltpu.CompilerParams(vmem_limit_bytes=56 * 1024 * 1024),
        interpret=interpret,
        name="feed_forward",
    )(table, order, rows, gathered)


def even_odd(values):
    rows, width = values.shape
    return values.reshape(rows, width // TILE, HALF, 2).swapaxes(2, 3).reshape(rows, width)


def group_side(members):
    side = 1
    while side * side < members:
        side *= 2
    return side


def gather_rows(values, groups):
    copies = jnp.broadcast_to(values[None], (len(groups[0]),) + values.shape)
    return lax.all_to_all(copies, "tensor", 0, 0, axis_index_groups=groups)


def exchange(keep, send, step, members):
    got = lax.ppermute(send, "tensor", [(t, t ^ step) for t in range(members)])
    return (keep.astype(jnp.float32) + got.astype(jnp.float32)).astype(jnp.bfloat16)


def reduce_stream(keep, send, blocks, steps, across, members):
    first, second = steps
    value = exchange(keep, send, first, members)
    half = value.shape[0] // 2
    value = exchange(value[:half], value[half:], second, members)
    size = value.shape[0] // len(ORDER)
    keep, send = (
        jnp.concatenate([value[block * size : (block + 1) * size] for block in chosen]) for chosen in blocks
    )
    value = exchange(keep, send, first * across, members)
    half = value.shape[0] // 2
    return exchange(value[:half], value[half:], second * across, members)


def local(tokens, norm_gain, gate_tiles, up_tiles, down_tiles, tile_ids, tile_counts):
    peers = lax.axis_size("dp")
    members = lax.axis_size("tensor")
    row_tiles = D // (TILE * peers)
    col_tiles = FF // (TILE * members)
    local_tiles = row_tiles * col_tiles
    slots = gate_tiles.shape[2]
    tiles = jnp.concatenate([gate_tiles[0, 0], up_tiles[0, 0], down_tiles[0, 0]], axis=0)
    gathered = lax.all_gather(tiles.reshape(3 * slots * HALF, LANES), "dp", axis=0)
    mine = even_odd(normalize(tokens, norm_gain))
    rows = mine.shape[0]
    across = group_side(members)
    along = members // across
    x_groups = [[y * across + x for x in range(across)] for y in range(along)]
    y_groups = [[y * across + x for y in range(along)] for x in range(across)]
    group_rows = gather_rows(mine, y_groups)
    entry = slot_table(tile_ids[0, 0], tile_counts[0, 0], local_tiles).reshape(1, 3 * local_tiles)
    entry = jnp.pad(entry, ((0, 0), (0, -entry.shape[1] % LANES)))
    entry, group_rows = lax.optimization_barrier((entry, group_rows))
    group_rows = gather_rows(group_rows.reshape(along * rows, D), x_groups).reshape(members * rows, D)
    table = lax.all_gather(entry, "dp", axis=0, tiled=True)
    assert across == along == len(ORDER)
    place_x, place_y = lax.axis_index("tensor") % across, lax.axis_index("tensor") // across
    offsets = jnp.asarray(ORDER, jnp.int32)
    order = (place_x ^ offsets)[:, None] * along + (place_y ^ offsets)[None, :]
    order = order.astype(jnp.int32).reshape(1, members)
    keep_1, send_1, keep_2, send_2 = apply_tiles(
        table, order, group_rows, gathered, slots=slots, row_tiles=row_tiles, col_tiles=col_tiles
    )
    first = reduce_stream(keep_1, send_1, BLOCKS[0], (1, 3), across, members)
    second = reduce_stream(keep_2, send_2, BLOCKS[1], (3, 1), across, members)
    return jnp.concatenate([first, second], axis=1)


def solution(mesh):
    return jax.shard_map(
        local,
        mesh=mesh,
        in_specs=(
            P(("dp", "tensor"), None),
            P(),
            P("tensor", "dp", None, None),
            P("tensor", "dp", None, None),
            P("tensor", "dp", None, None),
            P("tensor", "dp", None, None),
            P("tensor", "dp", None),
        ),
        out_specs=P(("dp", "tensor"), None),
        check_vma=False,
    )
```

```python
import functools

import jax
import jax.numpy as jnp
from jax import lax
from jax.experimental import pallas as pl
from jax.experimental.pallas import tpu as pltpu
from jax.sharding import PartitionSpec as P

D = 4096
FF = 14336
TILE = 64
HALF = TILE // 2
LANES = 2 * TILE
IN_PEERS = 4
OUT_PEERS = 4
ORDER = (0, 3, 1, 2)
BLOCKS = (((0, 1), (2, 3)), ((0, 2), (1, 3)))


def normalize(values, norm_gain):
    wide = values.astype(jnp.float32)
    meansq = jnp.mean(wide * wide, axis=-1, keepdims=True)
    return (wide * lax.rsqrt(meansq + 1e-05) * norm_gain).astype(jnp.bfloat16)


def slot_table(tile_ids, tile_counts, local_tiles, peer, peers):
    slots = tile_ids.shape[-1]
    order = jnp.arange(slots, dtype=jnp.int32)
    kept = order[None, :] < tile_counts[:, None]
    hit = (tile_ids[:, None, :] == jnp.arange(local_tiles)[None, :, None]) & kept[:, None, :]
    matrix = jnp.arange(3, dtype=jnp.int32)[:, None]
    stride = jnp.where(matrix == 2, slots, 2 * slots)
    slot = peer * stride + order[None, :] + slots * (matrix == 1)
    empty = peers * stride
    return empty + jnp.sum(jnp.where(hit, (slot - empty)[:, None, :], 0), axis=-1)


def place(tiles_ref, first, second):
    left = lax.broadcasted_iota(jnp.int32, (HALF, LANES), 1) < TILE
    one, two = tiles_ref[first], tiles_ref[second]
    even = jnp.where(left, one, pltpu.roll(two, TILE, 1))
    odd = jnp.where(left, pltpu.roll(one, TILE, 1), two)
    return even, odd


def join(blocks_ref):
    return jnp.concatenate([blocks_ref[block] for block in range(blocks_ref.shape[0])], axis=1)


class Copies:
    def __init__(self, gathered_ref, tiles_ref, sem_ref, peers, first, count):
        self.parts = (gathered_ref, tiles_ref, sem_ref, peers, first, count)

    def of(self, chunk):
        gathered_ref, tiles_ref, sem_ref, peers, first, count = self.parts
        for peer in (chunk * peers + step for step in range(peers)):
            yield pltpu.make_async_copy(
                gathered_ref.at[peer, pl.ds(first, count)], tiles_ref.at[pl.ds(peer * count, count)], sem_ref.at[peer]
            )

    def start(self, chunk):
        for copy in self.of(chunk):
            copy.start()

    def wait(self, chunk):
        for copy in self.of(chunk):
            copy.wait()


def feed_forward(table_ref, order_ref, tokens_ref, gathered_ref, *refs, peers, slots, row_tiles, col_tiles):
    out_refs, refs = refs[:4], refs[4:]
    rows_ref, tiles_ref, down_ref, gate_ref, up_ref, hidden_ref = refs[:6]
    inward_refs, outward_refs, token_sems, in_sems, out_sems = refs[6:8], refs[8:10], *refs[10:]
    local_tiles = row_tiles * col_tiles
    in_chunks = peers // IN_PEERS
    out_chunks = peers // OUT_PEERS
    in_rows = IN_PEERS * row_tiles * TILE
    out_lanes = OUT_PEERS * LANES
    members = token_sems.shape[0]
    size = rows_ref.shape[0] // members

    def token_copy(block):
        source = pl.ds(pl.multiple_of(order_ref[0, block] * size, size), size)
        return pltpu.make_async_copy(tokens_ref.at[source], rows_ref.at[pl.ds(block * size, size)], token_sems.at[block])

    inward_copy = Copies(gathered_ref, tiles_ref, in_sems, IN_PEERS, 0, 2 * slots)
    outward_copy = Copies(gathered_ref, down_ref, out_sems, OUT_PEERS, 2 * slots, slots)

    def inward_place(chunk, buffer):
        for local_peer in range(IN_PEERS):
            peer = chunk * IN_PEERS + local_peer
            for matrix in range(2):
                for row in range(row_tiles):
                    for col in range(0, col_tiles, 2):
                        entry = matrix * local_tiles + row * col_tiles + col
                        even, odd = place(tiles_ref, table_ref[peer, entry], table_ref[peer, entry + 1])
                        at = (local_peer * row_tiles + row) * TILE
                        buffer[matrix, col // 2, at : at + HALF, :] = even
                        buffer[matrix, col // 2, at + HALF : at + TILE, :] = odd

    def inward_multiply(chunk, buffer):
        rows = rows_ref[:, pl.ds(pl.multiple_of(chunk * in_rows, in_rows), in_rows)]
        gate_ref[...] += jnp.dot(rows, join(buffer.at[0]), preferred_element_type=jnp.float32)
        up_ref[...] += jnp.dot(rows, join(buffer.at[1]), preferred_element_type=jnp.float32)

    def outward_place(chunk, buffer):
        for local_peer in range(OUT_PEERS):
            peer = chunk * OUT_PEERS + local_peer
            for col in range(col_tiles):
                entry = 2 * local_tiles + col
                even, odd = place(down_ref, table_ref[peer, entry], table_ref[peer, entry + col_tiles])
                buffer[local_peer, col * TILE : col * TILE + HALF, :] = even
                buffer[local_peer, col * TILE + HALF : (col + 1) * TILE, :] = odd

    def outward_multiply(chunk, lane_chunk, buffer, keep_ref, send_ref, blocks):
        value = jnp.dot(hidden_ref[...], join(buffer), preferred_element_type=jnp.float32).astype(jnp.bfloat16)
        part = value.shape[0] // len(ORDER)
        at = pl.ds(pl.multiple_of(lane_chunk * out_lanes, out_lanes), out_lanes)
        for out_ref, chosen in zip((keep_ref, send_ref), blocks):
            for position, block in enumerate(chosen):
                out_ref[position * part : (position + 1) * part, at] = value[block * part : (block + 1) * part]

    inward_copy.start(0)
    for block in range(members):
        token_copy(block).start()
    inward_copy.start(1)
    inward_copy.start(2)
    tiles_ref[2 * slots * peers] = jnp.zeros((HALF, LANES), jnp.bfloat16)
    down_ref[slots * peers] = jnp.zeros((HALF, LANES), jnp.bfloat16)
    gate_ref[...] = jnp.zeros_like(gate_ref)
    up_ref[...] = jnp.zeros_like(up_ref)
    inward_copy.wait(0)
    inward_place(0, inward_refs[0])
    for block in range(members):
        token_copy(block).wait()

    def inward_pair(pair, carry):
        chunk = 2 * pair
        inward_copy.wait(chunk + 1)

        @pl.when(chunk + 2 < in_chunks)
        def next_chunk():
            inward_copy.wait(chunk + 2)

            @pl.when(chunk + 4 < in_chunks)
            def start_later():
                inward_copy.start(chunk + 3)
                inward_copy.start(chunk + 4)

            @pl.when(chunk + 4 >= in_chunks)
            def start_last():
                inward_copy.start(chunk + 3)
                for later in range(out_chunks):
                    outward_copy.start(later)

        inward_place(chunk + 1, inward_refs[1])
        inward_multiply(chunk, inward_refs[0])
        inward_place(jnp.minimum(chunk + 2, in_chunks - 1), inward_refs[0])
        inward_multiply(chunk + 1, inward_refs[1])
        return carry

    lax.fori_loop(0, in_chunks // 2, inward_pair, 0)

    source = lax.broadcasted_iota(jnp.int32, (LANES, LANES), 0)
    target = lax.broadcasted_iota(jnp.int32, (LANES, LANES), 1)
    inner = target % TILE
    wanted = target - inner + jnp.where(inner < HALF, 2 * inner, 2 * (inner - HALF) + 1)
    shuffle = (source == wanted).astype(jnp.bfloat16)
    outward_copy.wait(0)
    outward_place(0, outward_refs[0])
    for block in range(col_tiles // 2):
        lanes = slice(block * LANES, (block + 1) * LANES)
        value = (jax.nn.silu(gate_ref[:, lanes]) * up_ref[:, lanes]).astype(jnp.bfloat16)
        hidden_ref[:, lanes] = jnp.dot(value, shuffle, preferred_element_type=jnp.float32).astype(jnp.bfloat16)

    half = out_chunks // 2
    for stream in range(2):
        targets = (out_refs[2 * stream], out_refs[2 * stream + 1], BLOCKS[stream])

        def outward_pair(pair, carry):
            chunk = stream * half + 2 * pair
            outward_copy.wait(chunk + 1)

            @pl.when(chunk + 2 < out_chunks)
            def wait_next():
                outward_copy.wait(chunk + 2)

            outward_place(chunk + 1, outward_refs[1])
            outward_multiply(chunk, 2 * pair, outward_refs[0], *targets)
            outward_place(jnp.minimum(chunk + 2, out_chunks - 1), outward_refs[0])
            outward_multiply(chunk + 1, 2 * pair + 1, outward_refs[1], *targets)
            return carry

        lax.fori_loop(0, half // 2, outward_pair, 0)


SMEM = pl.BlockSpec(memory_space=pltpu.SMEM)
VMEM = pl.BlockSpec(memory_space=pltpu.VMEM)
ANY = pl.BlockSpec(memory_space=pl.ANY)


def apply_tiles(table, order, rows, gathered, *, slots, row_tiles, col_tiles, interpret=False):
    peers = gathered.shape[0]
    tokens, width = rows.shape
    hidden = col_tiles * TILE
    part = jax.ShapeDtypeStruct((tokens // 2, width // 2), jnp.bfloat16)
    inward = pltpu.VMEM((2, col_tiles // 2, IN_PEERS * row_tiles * TILE, LANES), jnp.bfloat16)
    outward = pltpu.VMEM((OUT_PEERS, hidden, LANES), jnp.bfloat16)
    return pl.pallas_call(
        functools.partial(feed_forward, peers=peers, slots=slots, row_tiles=row_tiles, col_tiles=col_tiles),
        out_shape=(part,) * 4,
        in_specs=[SMEM, SMEM, ANY, ANY],
        out_specs=(VMEM,) * 4,
        scratch_shapes=[
            pltpu.VMEM((tokens, width), jnp.bfloat16),
            pltpu.VMEM((2 * slots * peers + 1, HALF, LANES), jnp.bfloat16),
            pltpu.VMEM((slots * peers + 1, HALF, LANES), jnp.bfloat16),
            pltpu.VMEM((tokens, hidden), jnp.float32),
            pltpu.VMEM((tokens, hidden), jnp.float32),
            pltpu.VMEM((tokens, hidden), jnp.bfloat16),
            inward,
            inward,
            outward,
            outward,
            pltpu.SemaphoreType.DMA((order.shape[1],)),
            pltpu.SemaphoreType.DMA((peers,)),
            pltpu.SemaphoreType.DMA((peers,)),
        ],
        compiler_params=pltpu.CompilerParams(vmem_limit_bytes=56 * 1024 * 1024),
        interpret=interpret,
        name="feed_forward",
    )(table, order, rows, gathered)


def even_odd(values):
    rows, width = values.shape
    return values.reshape(rows, width // TILE, HALF, 2).swapaxes(2, 3).reshape(rows, width)


def group_side(members):
    side = 1
    while side * side < members:
        side *= 2
    return side


def gather_rows(values, groups):
    copies = jnp.broadcast_to(values[None], (len(groups[0]),) + values.shape)
    return lax.all_to_all(copies, "tensor", 0, 0, axis_index_groups=groups)


def exchange(keep, send, step, members):
    got = lax.ppermute(send, "tensor", [(t, t ^ step) for t in range(members)])
    return (keep.astype(jnp.float32) + got.astype(jnp.float32)).astype(jnp.bfloat16)


def reduce_stream(keep, send, blocks, steps, across, members):
    first, second = steps
    value = exchange(keep, send, first, members)
    half = value.shape[0] // 2
    value = exchange(value[:half], value[half:], second, members)
    size = value.shape[0] // len(ORDER)
    keep, send = (
        jnp.concatenate([value[block * size : (block + 1) * size] for block in chosen]) for chosen in blocks
    )
    value = exchange(keep, send, first * across, members)
    half = value.shape[0] // 2
    return exchange(value[:half], value[half:], second * across, members)


def local(tokens, norm_gain, gate_tiles, up_tiles, down_tiles, tile_ids, tile_counts):
    peers = lax.axis_size("dp")
    members = lax.axis_size("tensor")
    row_tiles = D // (TILE * peers)
    col_tiles = FF // (TILE * members)
    local_tiles = row_tiles * col_tiles
    slots = gate_tiles.shape[2]
    tiles = jnp.concatenate([gate_tiles[0, 0], up_tiles[0, 0], down_tiles[0, 0]], axis=0)
    gathered = lax.all_gather(tiles.reshape(3 * slots * HALF, LANES), "dp", axis=0)
    gathered = gathered.reshape(peers, 3 * slots, HALF, LANES)
    mine = even_odd(normalize(tokens, norm_gain))
    rows = mine.shape[0]
    across = group_side(members)
    along = members // across
    x_groups = [[y * across + x for x in range(across)] for y in range(along)]
    y_groups = [[y * across + x for y in range(along)] for x in range(across)]
    group_rows = gather_rows(mine, y_groups)
    entry = slot_table(tile_ids[0, 0], tile_counts[0, 0], local_tiles, lax.axis_index("dp"), peers).reshape(1, 3 * local_tiles)
    entry = jnp.pad(entry, ((0, 0), (0, -entry.shape[1] % LANES)))
    entry, group_rows = lax.optimization_barrier((entry, group_rows))
    group_rows = gather_rows(group_rows.reshape(along * rows, D), x_groups).reshape(members * rows, D)
    table = lax.all_gather(entry, "dp", axis=0, tiled=True)
    assert across == along == len(ORDER)
    place_x, place_y = lax.axis_index("tensor") % across, lax.axis_index("tensor") // across
    offsets = jnp.asarray(ORDER, jnp.int32)
    order = (place_x ^ offsets)[:, None] * along + (place_y ^ offsets)[None, :]
    order = order.astype(jnp.int32).reshape(1, members)
    keep_1, send_1, keep_2, send_2 = apply_tiles(
        table, order, group_rows, gathered, slots=slots, row_tiles=row_tiles, col_tiles=col_tiles
    )
    first = reduce_stream(keep_1, send_1, BLOCKS[0], (1, 3), across, members)
    second = reduce_stream(keep_2, send_2, BLOCKS[1], (3, 1), across, members)
    return jnp.concatenate([first, second], axis=1)


def solution(mesh):
    return jax.shard_map(
        local,
        mesh=mesh,
        in_specs=(
            P(("dp", "tensor"), None),
            P(),
            P("tensor", "dp", None, None),
            P("tensor", "dp", None, None),
            P("tensor", "dp", None, None),
            P("tensor", "dp", None, None),
            P("tensor", "dp", None),
        ),
        out_specs=P(("dp", "tensor"), None),
        check_vma=False,
    )
```

```python
import functools

import jax
import jax.numpy as jnp
from jax import lax
from jax.experimental import pallas as pl
from jax.experimental.pallas import tpu as pltpu
from jax.sharding import PartitionSpec as P

D = 4096
FF = 14336
TILE = 64
HALF = TILE // 2
LANES = 2 * TILE
IN_PEERS = 4
OUT_PEERS = 4
SIDE = 4


def normalize(values, norm_gain):
    wide = values.astype(jnp.float32)
    meansq = jnp.mean(wide * wide, axis=-1, keepdims=True)
    return (wide * lax.rsqrt(meansq + 1e-05) * norm_gain).astype(jnp.bfloat16)


def slot_table(tile_ids, tile_counts, local_tiles, peer, peers):
    slots = tile_ids.shape[-1]
    order = jnp.arange(slots, dtype=jnp.int32)
    kept = order[None, :] < tile_counts[:, None]
    hit = (tile_ids[:, None, :] == jnp.arange(local_tiles)[None, :, None]) & kept[:, None, :]
    matrix = jnp.arange(3, dtype=jnp.int32)[:, None]
    stride = jnp.where(matrix == 2, slots, 2 * slots)
    slot = peer * stride + order[None, :] + slots * (matrix == 1)
    empty = peers * stride
    return empty + jnp.sum(jnp.where(hit, (slot - empty)[:, None, :], 0), axis=-1)


def place(tiles_ref, first, second):
    left = lax.broadcasted_iota(jnp.int32, (HALF, LANES), 1) < TILE
    one, two = tiles_ref[first], tiles_ref[second]
    even = jnp.where(left, one, pltpu.roll(two, TILE, 1))
    odd = jnp.where(left, pltpu.roll(one, TILE, 1), two)
    return even, odd


def join(blocks_ref):
    return jnp.concatenate([blocks_ref[block] for block in range(blocks_ref.shape[0])], axis=1)


class Copies:
    def __init__(self, gathered_ref, tiles_ref, sem_ref, peers, first, count):
        self.parts = (gathered_ref, tiles_ref, sem_ref, peers, first, count)

    def of(self, chunk):
        gathered_ref, tiles_ref, sem_ref, peers, first, count = self.parts
        for peer in (chunk * peers + step for step in range(peers)):
            yield pltpu.make_async_copy(
                gathered_ref.at[peer, pl.ds(first, count)], tiles_ref.at[pl.ds(peer * count, count)], sem_ref.at[peer]
            )

    def start(self, chunk):
        for copy in self.of(chunk):
            copy.start()

    def wait(self, chunk):
        for copy in self.of(chunk):
            copy.wait()


def feed_forward(table_ref, order_ref, tokens_ref, gathered_ref, *refs, peers, slots, row_tiles, col_tiles):
    out_refs, refs = refs[:SIDE], refs[SIDE:]
    rows_ref, tiles_ref, down_ref, gate_ref, up_ref, hidden_ref = refs[:6]
    inward_refs, outward_refs, token_sems, in_sems, out_sems = refs[6:8], refs[8:10], *refs[10:]
    local_tiles = row_tiles * col_tiles
    in_chunks = peers // IN_PEERS
    out_chunks = peers // OUT_PEERS
    in_rows = IN_PEERS * row_tiles * TILE
    out_lanes = OUT_PEERS * LANES
    members = token_sems.shape[0]
    size = rows_ref.shape[0] // members

    def token_copy(block):
        source = pl.ds(pl.multiple_of(order_ref[0, block] * size, size), size)
        return pltpu.make_async_copy(tokens_ref.at[source], rows_ref.at[pl.ds(block * size, size)], token_sems.at[block])

    inward_copy = Copies(gathered_ref, tiles_ref, in_sems, IN_PEERS, 0, 2 * slots)
    outward_copy = Copies(gathered_ref, down_ref, out_sems, OUT_PEERS, 2 * slots, slots)

    def inward_place(chunk, buffer):
        for local_peer in range(IN_PEERS):
            peer = chunk * IN_PEERS + local_peer
            for matrix in range(2):
                for row in range(row_tiles):
                    for col in range(0, col_tiles, 2):
                        entry = matrix * local_tiles + row * col_tiles + col
                        even, odd = place(tiles_ref, table_ref[peer, entry], table_ref[peer, entry + 1])
                        at = (local_peer * row_tiles + row) * TILE
                        buffer[matrix, col // 2, at : at + HALF, :] = even
                        buffer[matrix, col // 2, at + HALF : at + TILE, :] = odd

    def inward_multiply(chunk, buffer):
        rows = rows_ref[:, pl.ds(pl.multiple_of(chunk * in_rows, in_rows), in_rows)]
        gate_ref[...] += jnp.dot(rows, join(buffer.at[0]), preferred_element_type=jnp.float32)
        up_ref[...] += jnp.dot(rows, join(buffer.at[1]), preferred_element_type=jnp.float32)

    def outward_place(chunk, buffer):
        for local_peer in range(OUT_PEERS):
            peer = chunk * OUT_PEERS + local_peer
            for col in range(col_tiles):
                entry = 2 * local_tiles + col
                even, odd = place(down_ref, table_ref[peer, entry], table_ref[peer, entry + col_tiles])
                buffer[local_peer, col * TILE : col * TILE + HALF, :] = even
                buffer[local_peer, col * TILE + HALF : (col + 1) * TILE, :] = odd

    def outward_multiply(chunk, buffer):
        value = jnp.dot(hidden_ref[...], join(buffer), preferred_element_type=jnp.float32).astype(jnp.bfloat16)
        part = value.shape[0] // SIDE
        at = pl.ds(pl.multiple_of(chunk * out_lanes, out_lanes), out_lanes)
        for block, out_ref in enumerate(out_refs):
            out_ref[:, at] = value[block * part : (block + 1) * part]

    inward_copy.start(0)
    for block in range(members):
        token_copy(block).start()
    inward_copy.start(1)
    inward_copy.start(2)
    tiles_ref[2 * slots * peers] = jnp.zeros((HALF, LANES), jnp.bfloat16)
    down_ref[slots * peers] = jnp.zeros((HALF, LANES), jnp.bfloat16)
    gate_ref[...] = jnp.zeros_like(gate_ref)
    up_ref[...] = jnp.zeros_like(up_ref)
    inward_copy.wait(0)
    inward_place(0, inward_refs[0])
    for block in range(members):
        token_copy(block).wait()

    def inward_pair(pair, carry):
        chunk = 2 * pair
        inward_copy.wait(chunk + 1)

        @pl.when(chunk + 2 < in_chunks)
        def next_chunk():
            inward_copy.wait(chunk + 2)

            @pl.when(chunk + 4 < in_chunks)
            def start_later():
                inward_copy.start(chunk + 3)
                inward_copy.start(chunk + 4)

            @pl.when(chunk + 4 >= in_chunks)
            def start_last():
                inward_copy.start(chunk + 3)
                for later in range(out_chunks):
                    outward_copy.start(later)

        inward_place(chunk + 1, inward_refs[1])
        inward_multiply(chunk, inward_refs[0])
        inward_place(jnp.minimum(chunk + 2, in_chunks - 1), inward_refs[0])
        inward_multiply(chunk + 1, inward_refs[1])
        return carry

    lax.fori_loop(0, in_chunks // 2, inward_pair, 0)

    source = lax.broadcasted_iota(jnp.int32, (LANES, LANES), 0)
    target = lax.broadcasted_iota(jnp.int32, (LANES, LANES), 1)
    inner = target % TILE
    wanted = target - inner + jnp.where(inner < HALF, 2 * inner, 2 * (inner - HALF) + 1)
    shuffle = (source == wanted).astype(jnp.bfloat16)
    outward_copy.wait(0)
    outward_place(0, outward_refs[0])
    for block in range(col_tiles // 2):
        lanes = slice(block * LANES, (block + 1) * LANES)
        value = (jax.nn.silu(gate_ref[:, lanes]) * up_ref[:, lanes]).astype(jnp.bfloat16)
        hidden_ref[:, lanes] = jnp.dot(value, shuffle, preferred_element_type=jnp.float32).astype(jnp.bfloat16)

    def outward_pair(pair, carry):
        chunk = 2 * pair
        outward_copy.wait(chunk + 1)

        @pl.when(chunk + 2 < out_chunks)
        def wait_next():
            outward_copy.wait(chunk + 2)

        outward_place(chunk + 1, outward_refs[1])
        outward_multiply(chunk, outward_refs[0])
        outward_place(jnp.minimum(chunk + 2, out_chunks - 1), outward_refs[0])
        outward_multiply(chunk + 1, outward_refs[1])
        return carry

    lax.fori_loop(0, out_chunks // 2, outward_pair, 0)


SMEM = pl.BlockSpec(memory_space=pltpu.SMEM)
VMEM = pl.BlockSpec(memory_space=pltpu.VMEM)
ANY = pl.BlockSpec(memory_space=pl.ANY)


def apply_tiles(table, order, rows, gathered, *, slots, row_tiles, col_tiles, interpret=False):
    peers = gathered.shape[0]
    tokens, width = rows.shape
    hidden = col_tiles * TILE
    part = jax.ShapeDtypeStruct((tokens // SIDE, width), jnp.bfloat16)
    inward = pltpu.VMEM((2, col_tiles // 2, IN_PEERS * row_tiles * TILE, LANES), jnp.bfloat16)
    outward = pltpu.VMEM((OUT_PEERS, hidden, LANES), jnp.bfloat16)
    return pl.pallas_call(
        functools.partial(feed_forward, peers=peers, slots=slots, row_tiles=row_tiles, col_tiles=col_tiles),
        out_shape=(part,) * SIDE,
        in_specs=[SMEM, SMEM, ANY, ANY],
        out_specs=(VMEM,) * SIDE,
        scratch_shapes=[
            pltpu.VMEM((tokens, width), jnp.bfloat16),
            pltpu.VMEM((2 * slots * peers + 1, HALF, LANES), jnp.bfloat16),
            pltpu.VMEM((slots * peers + 1, HALF, LANES), jnp.bfloat16),
            pltpu.VMEM((tokens, hidden), jnp.float32),
            pltpu.VMEM((tokens, hidden), jnp.float32),
            pltpu.VMEM((tokens, hidden), jnp.bfloat16),
            inward,
            inward,
            outward,
            outward,
            pltpu.SemaphoreType.DMA((order.shape[1],)),
            pltpu.SemaphoreType.DMA((peers,)),
            pltpu.SemaphoreType.DMA((peers,)),
        ],
        compiler_params=pltpu.CompilerParams(vmem_limit_bytes=56 * 1024 * 1024),
        interpret=interpret,
        name="feed_forward",
    )(table, order, rows, gathered)


def even_odd(values):
    rows, width = values.shape
    return values.reshape(rows, width // TILE, HALF, 2).swapaxes(2, 3).reshape(rows, width)


def group_side(members):
    side = 1
    while side * side < members:
        side *= 2
    return side


def gather_rows(values, groups):
    copies = jnp.broadcast_to(values[None], (len(groups[0]),) + values.shape)
    return lax.all_to_all(copies, "tensor", 0, 0, axis_index_groups=groups)


def reduce_places(parts, step, members):
    total = parts[0].astype(jnp.float32)
    for offset in (2, 1, 3):
        pairs = [(t, t ^ (offset * step)) for t in range(members)]
        total = total + lax.ppermute(parts[offset], "tensor", pairs).astype(jnp.float32)
    return total.astype(jnp.bfloat16)


def local(tokens, norm_gain, gate_tiles, up_tiles, down_tiles, tile_ids, tile_counts):
    peers = lax.axis_size("dp")
    members = lax.axis_size("tensor")
    row_tiles = D // (TILE * peers)
    col_tiles = FF // (TILE * members)
    local_tiles = row_tiles * col_tiles
    slots = gate_tiles.shape[2]
    tiles = jnp.concatenate([gate_tiles[0, 0], up_tiles[0, 0], down_tiles[0, 0]], axis=0)
    gathered = lax.all_gather(tiles.reshape(3 * slots * HALF, LANES), "dp", axis=0)
    gathered = gathered.reshape(peers, 3 * slots, HALF, LANES)
    mine = even_odd(normalize(tokens, norm_gain))
    rows = mine.shape[0]
    across = group_side(members)
    along = members // across
    x_groups = [[y * across + x for x in range(across)] for y in range(along)]
    y_groups = [[y * across + x for y in range(along)] for x in range(across)]
    group_rows = gather_rows(mine, y_groups)
    entry = slot_table(tile_ids[0, 0], tile_counts[0, 0], local_tiles, lax.axis_index("dp"), peers).reshape(1, 3 * local_tiles)
    entry = jnp.pad(entry, ((0, 0), (0, -entry.shape[1] % LANES)))
    entry, group_rows = lax.optimization_barrier((entry, group_rows))
    group_rows = gather_rows(group_rows.reshape(along * rows, D), x_groups).reshape(members * rows, D)
    table = lax.all_gather(entry, "dp", axis=0, tiled=True)
    assert across == along == SIDE
    place_x, place_y = lax.axis_index("tensor") % across, lax.axis_index("tensor") // across
    offsets = jnp.arange(SIDE, dtype=jnp.int32)
    order = (place_x ^ offsets)[:, None] * along + (place_y ^ offsets)[None, :]
    order = order.astype(jnp.int32).reshape(1, members)
    parts = apply_tiles(
        table, order, group_rows, gathered, slots=slots, row_tiles=row_tiles, col_tiles=col_tiles
    )
    summed = reduce_places(parts, 1, members)
    return reduce_places([summed[k * rows : (k + 1) * rows] for k in range(SIDE)], across, members)


def solution(mesh):
    return jax.shard_map(
        local,
        mesh=mesh,
        in_specs=(
            P(("dp", "tensor"), None),
            P(),
            P("tensor", "dp", None, None),
            P("tensor", "dp", None, None),
            P("tensor", "dp", None, None),
            P("tensor", "dp", None, None),
            P("tensor", "dp", None),
        ),
        out_specs=P(("dp", "tensor"), None),
        check_vma=False,
    )
```

```python
import functools

import jax
import jax.numpy as jnp
from jax import lax
from jax.experimental import pallas as pl
from jax.experimental.pallas import tpu as pltpu
from jax.sharding import PartitionSpec as P

D = 4096
FF = 14336
TILE = 64
HALF = TILE // 2
LANES = 2 * TILE
IN_PEERS = 4
OUT_PEERS = 4
SIDE = 4
STREAMS = 2


def normalize(values, norm_gain):
    wide = values.astype(jnp.float32)
    meansq = jnp.mean(wide * wide, axis=-1, keepdims=True)
    return (wide * lax.rsqrt(meansq + 1e-05) * norm_gain).astype(jnp.bfloat16)


def slot_table(tile_ids, tile_counts, local_tiles, peer, peers):
    slots = tile_ids.shape[-1]
    order = jnp.arange(slots, dtype=jnp.int32)
    kept = order[None, :] < tile_counts[:, None]
    hit = (tile_ids[:, None, :] == jnp.arange(local_tiles)[None, :, None]) & kept[:, None, :]
    matrix = jnp.arange(3, dtype=jnp.int32)[:, None]
    stride = jnp.where(matrix == 2, slots, 2 * slots)
    slot = peer * stride + order[None, :] + slots * (matrix == 1)
    empty = peers * stride
    return empty + jnp.sum(jnp.where(hit, (slot - empty)[:, None, :], 0), axis=-1)


def place(tiles_ref, first, second):
    left = lax.broadcasted_iota(jnp.int32, (HALF, LANES), 1) < TILE
    one, two = tiles_ref[first], tiles_ref[second]
    even = jnp.where(left, one, pltpu.roll(two, TILE, 1))
    odd = jnp.where(left, pltpu.roll(one, TILE, 1), two)
    return even, odd


def join(blocks_ref):
    return jnp.concatenate([blocks_ref[block] for block in range(blocks_ref.shape[0])], axis=1)


class Copies:
    def __init__(self, gathered_ref, tiles_ref, sem_ref, peers, first, count):
        self.parts = (gathered_ref, tiles_ref, sem_ref, peers, first, count)

    def of(self, chunk):
        gathered_ref, tiles_ref, sem_ref, peers, first, count = self.parts
        for peer in (chunk * peers + step for step in range(peers)):
            yield pltpu.make_async_copy(
                gathered_ref.at[peer, pl.ds(first, count)], tiles_ref.at[pl.ds(peer * count, count)], sem_ref.at[peer]
            )

    def start(self, chunk):
        for copy in self.of(chunk):
            copy.start()

    def wait(self, chunk):
        for copy in self.of(chunk):
            copy.wait()


def feed_forward(table_ref, order_ref, tokens_ref, gathered_ref, *refs, peers, slots, row_tiles, col_tiles):
    out_refs, refs = refs[: STREAMS * SIDE], refs[STREAMS * SIDE :]
    rows_ref, tiles_ref, down_ref, gate_ref, up_ref, hidden_ref = refs[:6]
    inward_refs, outward_refs, token_sems, in_sems, out_sems = refs[6:8], refs[8:10], *refs[10:]
    local_tiles = row_tiles * col_tiles
    in_chunks = peers // IN_PEERS
    out_chunks = peers // OUT_PEERS
    in_rows = IN_PEERS * row_tiles * TILE
    out_lanes = OUT_PEERS * LANES
    members = token_sems.shape[0]
    size = rows_ref.shape[0] // members

    def token_copy(block):
        source = pl.ds(pl.multiple_of(order_ref[0, block] * size, size), size)
        return pltpu.make_async_copy(tokens_ref.at[source], rows_ref.at[pl.ds(block * size, size)], token_sems.at[block])

    inward_copy = Copies(gathered_ref, tiles_ref, in_sems, IN_PEERS, 0, 2 * slots)
    outward_copy = Copies(gathered_ref, down_ref, out_sems, OUT_PEERS, 2 * slots, slots)

    def inward_place(chunk, buffer):
        for local_peer in range(IN_PEERS):
            peer = chunk * IN_PEERS + local_peer
            for matrix in range(2):
                for row in range(row_tiles):
                    for col in range(0, col_tiles, 2):
                        entry = matrix * local_tiles + row * col_tiles + col
                        even, odd = place(tiles_ref, table_ref[peer, entry], table_ref[peer, entry + 1])
                        at = (local_peer * row_tiles + row) * TILE
                        buffer[matrix, col // 2, at : at + HALF, :] = even
                        buffer[matrix, col // 2, at + HALF : at + TILE, :] = odd

    def inward_multiply(chunk, buffer):
        rows = rows_ref[:, pl.ds(pl.multiple_of(chunk * in_rows, in_rows), in_rows)]
        gate_ref[...] += jnp.dot(rows, join(buffer.at[0]), preferred_element_type=jnp.float32)
        up_ref[...] += jnp.dot(rows, join(buffer.at[1]), preferred_element_type=jnp.float32)

    def outward_place(chunk, buffer):
        for local_peer in range(OUT_PEERS):
            peer = chunk * OUT_PEERS + local_peer
            for col in range(col_tiles):
                entry = 2 * local_tiles + col
                even, odd = place(down_ref, table_ref[peer, entry], table_ref[peer, entry + col_tiles])
                buffer[local_peer, col * TILE : col * TILE + HALF, :] = even
                buffer[local_peer, col * TILE + HALF : (col + 1) * TILE, :] = odd

    def outward_multiply(chunk, lane_chunk, buffer, targets):
        value = jnp.dot(hidden_ref[...], join(buffer), preferred_element_type=jnp.float32).astype(jnp.bfloat16)
        part = value.shape[0] // SIDE
        at = pl.ds(pl.multiple_of(lane_chunk * out_lanes, out_lanes), out_lanes)
        for block, out_ref in enumerate(targets):
            out_ref[:, at] = value[block * part : (block + 1) * part]

    inward_copy.start(0)
    for block in range(members):
        token_copy(block).start()
    inward_copy.start(1)
    inward_copy.start(2)
    tiles_ref[2 * slots * peers] = jnp.zeros((HALF, LANES), jnp.bfloat16)
    down_ref[slots * peers] = jnp.zeros((HALF, LANES), jnp.bfloat16)
    gate_ref[...] = jnp.zeros_like(gate_ref)
    up_ref[...] = jnp.zeros_like(up_ref)
    inward_copy.wait(0)
    inward_place(0, inward_refs[0])
    for block in range(members):
        token_copy(block).wait()

    def inward_pair(pair, carry):
        chunk = 2 * pair
        inward_copy.wait(chunk + 1)

        @pl.when(chunk + 2 < in_chunks)
        def next_chunk():
            inward_copy.wait(chunk + 2)

            @pl.when(chunk + 4 < in_chunks)
            def start_later():
                inward_copy.start(chunk + 3)
                inward_copy.start(chunk + 4)

            @pl.when(chunk + 4 >= in_chunks)
            def start_last():
                inward_copy.start(chunk + 3)
                for later in range(out_chunks):
                    outward_copy.start(later)

        inward_place(chunk + 1, inward_refs[1])
        inward_multiply(chunk, inward_refs[0])
        inward_place(jnp.minimum(chunk + 2, in_chunks - 1), inward_refs[0])
        inward_multiply(chunk + 1, inward_refs[1])
        return carry

    lax.fori_loop(0, in_chunks // 2, inward_pair, 0)

    source = lax.broadcasted_iota(jnp.int32, (LANES, LANES), 0)
    target = lax.broadcasted_iota(jnp.int32, (LANES, LANES), 1)
    inner = target % TILE
    wanted = target - inner + jnp.where(inner < HALF, 2 * inner, 2 * (inner - HALF) + 1)
    shuffle = (source == wanted).astype(jnp.bfloat16)
    outward_copy.wait(0)
    outward_place(0, outward_refs[0])
    for block in range(col_tiles // 2):
        lanes = slice(block * LANES, (block + 1) * LANES)
        value = (jax.nn.silu(gate_ref[:, lanes]) * up_ref[:, lanes]).astype(jnp.bfloat16)
        hidden_ref[:, lanes] = jnp.dot(value, shuffle, preferred_element_type=jnp.float32).astype(jnp.bfloat16)

    half = out_chunks // STREAMS
    for stream in range(STREAMS):
        targets = out_refs[stream * SIDE : (stream + 1) * SIDE]

        def outward_pair(pair, carry):
            chunk = stream * half + 2 * pair
            outward_copy.wait(chunk + 1)

            @pl.when(chunk + 2 < out_chunks)
            def wait_next():
                outward_copy.wait(chunk + 2)

            outward_place(chunk + 1, outward_refs[1])
            outward_multiply(chunk, 2 * pair, outward_refs[0], targets)
            outward_place(jnp.minimum(chunk + 2, out_chunks - 1), outward_refs[0])
            outward_multiply(chunk + 1, 2 * pair + 1, outward_refs[1], targets)
            return carry

        lax.fori_loop(0, half // 2, outward_pair, 0)


SMEM = pl.BlockSpec(memory_space=pltpu.SMEM)
VMEM = pl.BlockSpec(memory_space=pltpu.VMEM)
ANY = pl.BlockSpec(memory_space=pl.ANY)


def apply_tiles(table, order, rows, gathered, *, slots, row_tiles, col_tiles, interpret=False):
    peers = gathered.shape[0]
    tokens, width = rows.shape
    hidden = col_tiles * TILE
    part = jax.ShapeDtypeStruct((tokens // SIDE, width // STREAMS), jnp.bfloat16)
    inward = pltpu.VMEM((2, col_tiles // 2, IN_PEERS * row_tiles * TILE, LANES), jnp.bfloat16)
    outward = pltpu.VMEM((OUT_PEERS, hidden, LANES), jnp.bfloat16)
    return pl.pallas_call(
        functools.partial(feed_forward, peers=peers, slots=slots, row_tiles=row_tiles, col_tiles=col_tiles),
        out_shape=(part,) * (STREAMS * SIDE),
        in_specs=[SMEM, SMEM, ANY, ANY],
        out_specs=(VMEM,) * (STREAMS * SIDE),
        scratch_shapes=[
            pltpu.VMEM((tokens, width), jnp.bfloat16),
            pltpu.VMEM((2 * slots * peers + 1, HALF, LANES), jnp.bfloat16),
            pltpu.VMEM((slots * peers + 1, HALF, LANES), jnp.bfloat16),
            pltpu.VMEM((tokens, hidden), jnp.float32),
            pltpu.VMEM((tokens, hidden), jnp.float32),
            pltpu.VMEM((tokens, hidden), jnp.bfloat16),
            inward,
            inward,
            outward,
            outward,
            pltpu.SemaphoreType.DMA((order.shape[1],)),
            pltpu.SemaphoreType.DMA((peers,)),
            pltpu.SemaphoreType.DMA((peers,)),
        ],
        compiler_params=pltpu.CompilerParams(vmem_limit_bytes=56 * 1024 * 1024),
        interpret=interpret,
        name="feed_forward",
    )(table, order, rows, gathered)


def even_odd(values):
    rows, width = values.shape
    return values.reshape(rows, width // TILE, HALF, 2).swapaxes(2, 3).reshape(rows, width)


def group_side(members):
    side = 1
    while side * side < members:
        side *= 2
    return side


def gather_rows(values, groups):
    copies = jnp.broadcast_to(values[None], (len(groups[0]),) + values.shape)
    return lax.all_to_all(copies, "tensor", 0, 0, axis_index_groups=groups)


def reduce_places(parts, step, members):
    total = parts[0].astype(jnp.float32)
    for offset in (2, 1, 3):
        pairs = [(t, t ^ (offset * step)) for t in range(members)]
        total = total + lax.ppermute(parts[offset], "tensor", pairs).astype(jnp.float32)
    return total.astype(jnp.bfloat16)


def local(tokens, norm_gain, gate_tiles, up_tiles, down_tiles, tile_ids, tile_counts):
    peers = lax.axis_size("dp")
    members = lax.axis_size("tensor")
    row_tiles = D // (TILE * peers)
    col_tiles = FF // (TILE * members)
    local_tiles = row_tiles * col_tiles
    slots = gate_tiles.shape[2]
    tiles = jnp.concatenate([gate_tiles[0, 0], up_tiles[0, 0], down_tiles[0, 0]], axis=0)
    gathered = lax.all_gather(tiles.reshape(3 * slots * HALF, LANES), "dp", axis=0)
    gathered = gathered.reshape(peers, 3 * slots, HALF, LANES)
    mine = even_odd(normalize(tokens, norm_gain))
    rows = mine.shape[0]
    across = group_side(members)
    along = members // across
    x_groups = [[y * across + x for x in range(across)] for y in range(along)]
    y_groups = [[y * across + x for y in range(along)] for x in range(across)]
    group_rows = gather_rows(mine, y_groups)
    entry = slot_table(tile_ids[0, 0], tile_counts[0, 0], local_tiles, lax.axis_index("dp"), peers).reshape(1, 3 * local_tiles)
    entry = jnp.pad(entry, ((0, 0), (0, -entry.shape[1] % LANES)))
    entry, group_rows = lax.optimization_barrier((entry, group_rows))
    group_rows = gather_rows(group_rows.reshape(along * rows, D), x_groups).reshape(members * rows, D)
    table = lax.all_gather(entry, "dp", axis=0, tiled=True)
    assert across == along == SIDE
    place_x, place_y = lax.axis_index("tensor") % across, lax.axis_index("tensor") // across
    offsets = jnp.arange(SIDE, dtype=jnp.int32)
    order = (place_x ^ offsets)[:, None] * along + (place_y ^ offsets)[None, :]
    order = order.astype(jnp.int32).reshape(1, members)
    parts = apply_tiles(
        table, order, group_rows, gathered, slots=slots, row_tiles=row_tiles, col_tiles=col_tiles
    )
    streams = []
    for stream in range(STREAMS):
        summed = reduce_places(parts[stream * SIDE : (stream + 1) * SIDE], 1, members)
        places = [summed[k * rows : (k + 1) * rows] for k in range(SIDE)]
        streams.append(reduce_places(places, across, members))
    return jnp.concatenate(streams, axis=1)


def solution(mesh):
    return jax.shard_map(
        local,
        mesh=mesh,
        in_specs=(
            P(("dp", "tensor"), None),
            P(),
            P("tensor", "dp", None, None),
            P("tensor", "dp", None, None),
            P("tensor", "dp", None, None),
            P("tensor", "dp", None, None),
            P("tensor", "dp", None),
        ),
        out_specs=P(("dp", "tensor"), None),
        check_vma=False,
    )
```
